512 devices in a mesh: ep: 64 (over y, x, core), tp: 8 (over z).
Axes of the slice: x: 4, y: 8, z: 8, core: 2. Of those that a mesh axis runs over, the one named last changes fastest.
Arguments:
- tokens: bfloat16 [8192, 2048], P('ep', 'tp'), may hold values from -6 to 6
- cotangent: bfloat16 [8192, 2048], P('ep', 'tp'), may hold values from -6 to 6
- expert_ids: int32 [8192, 6], P('ep'), may hold values from 0 to 63, all different within a row; in each aligned block of 128 rows (0 to 127, 128 to 255, ...) at most 16 rows name the same one
- gate_values: float32 [8192, 6], P('ep'), may hold values from 0.1 to 1
- w_gate: bfloat16 [64, 1408, 2048], P('ep', 'tp'), may hold values from -0.125 to 0.125
- w_up: bfloat16 [64, 1408, 2048], P('ep', 'tp'), may hold values from -0.125 to 0.125
- w_down: bfloat16 [64, 1408, 2048], P('ep', 'tp'), may hold values from -0.15625 to 0.15625
Outputs:
- input_grad: bfloat16 [8192, 2048], P('ep', 'tp')
- grad_gate: bfloat16 [64, 1408, 2048], P('ep', 'tp')
- grad_up: bfloat16 [64, 1408, 2048], P('ep', 'tp')
- grad_down: bfloat16 [64, 1408, 2048], P('ep', 'tp')
The draws below stay inside these ranges and needn't reach their ends.
Inputs may be any that keep to these rules, and one draw needn't show every extreme that they name: `expert_ids`: each token names 6 different experts. Among the 128 tokens of one group, no expert is named more than 16 times.
All inputs are finite; a program needn't handle non-finite values.
Results may differ from the reference program's by a relative error of at most 0.017.
Values may be sent and summed in bfloat16 or wider, within the bound.
No kernel may reach another device: no remote copies, remote signals or barrier semaphores. Data moves between devices by JAX's collectives and lax.ppermute only.
A program may use at most 64 MiB of HBM per device.

```python
import math
from functools import partial
import jax
import jax.numpy as jnp
import numpy as np
from jax import lax

D = 2048
FF = 1408
TOP = 6
TOK_DEV = 128
EXPERTS = 64
CAP = 16
TOKENS = 8192
N_EP = 64
N_TP = 8


def block_levels(stream_key, extent, cuts, low, high):
    def one(axis_at, shards_of):
        heights = jax.random.uniform(jax.random.fold_in(jax.random.fold_in(stream_key, 6), axis_at), (shards_of,), jnp.float32, low / len(cuts), high / len(cuts))
        return jnp.repeat(jnp.exp(heights), extent[axis_at] // shards_of).reshape((-1,) + (1,) * (len(extent) - axis_at - 1))

    gain = one(*cuts[0])
    for cut in cuts[1:]:
        gain = gain * one(*cut)
    return gain


def assign_block(key, own, number, rows, amount, top, bound, skew):
    ranking = jax.random.permutation(key, amount)
    packed, usual = load_shares(amount, rows * top, bound, skew, True), load_shares(amount, rows * top, bound, skew, False)
    places = jnp.arange(amount)

    def named(lengths, turn):
        used = int((lengths > 0).sum())
        fixed = max(1, used // 4)
        moved = fixed + (places - fixed + turn * (used - fixed)) % max(1, amount - fixed)
        return jnp.zeros((amount,), jnp.int32).at[ranking[jnp.where(places < fixed, places, moved)]].set(jnp.asarray(lengths, jnp.int32))

    lengths = jnp.where(number % 4 == 0, named(packed, number // 4), named(usual, number - number // 4 - 1))
    mixed = jax.random.permutation(jax.random.fold_in(own, 3), amount)
    giver, taker = mixed[0:amount // 2 * 2:2], mixed[1:amount // 2 * 2:2]
    slack = jnp.minimum(lengths[giver] - 1, bound - lengths[taker]) // 2
    slack = jnp.where((giver == ranking[0]) | (taker == ranking[0]) | (lengths[taker] == 0), 0, jnp.maximum(slack, 0))
    moved = jax.random.randint(jax.random.fold_in(own, 4), (amount // 2,), 0, 1 << 20) % (slack + 1)
    lengths = lengths.at[giver].add(-moved).at[taker].add(moved)
    items = jnp.searchsorted(jnp.cumsum(lengths), jnp.arange(rows * top), side="right").astype(jnp.int32)
    grid = items.reshape(top, rows).T
    grid = grid[jax.random.permutation(jax.random.fold_in(own, 1), rows)]
    turn = jax.random.randint(jax.random.fold_in(own, 2), (rows, 1), 0, top)
    return jnp.take_along_axis(grid, (jnp.arange(top)[None, :] + turn) % top, axis=1)


def load_shares(count, total, reach, lean, full):
    loads = [(1 << 20) // math.isqrt(standing ** lean) + 1 for standing in range(1, count + 1)]
    largest = reach if full else min(reach, max(-(-total // count), total * loads[0] // sum(loads)))
    least = 1 if total - largest >= count - 1 else 0
    holding, spare = [largest] + [least] * (count - 1), total - largest - least * (count - 1)
    while spare > 0:
        movable = [i for i in range(1, count) if holding[i] < largest] or [i for i in range(1, count) if holding[i] < reach]
        whole, budget = sum([loads[i] for i in movable]), spare
        for i in movable:
            addition = min(reach - holding[i], max(1, budget * loads[i] // whole), spare)
            holding[i] = holding[i] + addition
            spare = spare - addition
    return np.array(holding)


def scatter_about(rng, extent, deviation, reach, pieces=(), kind=jnp.bfloat16):
    result = jax.random.normal(rng, extent, jnp.float32) * deviation
    if len(pieces) > 0:
        result = block_levels(rng, extent, pieces, -0.22, 0.18) * result
    return jnp.clip(result, min=-reach, max=reach).astype(kind)


def setup_inputs(seed: int = 0) -> dict:
    streams_of = jax.random.split(jax.random.key(seed), 8)
    tokens = scatter_about(streams_of[0], (TOKENS, D), 1.0, 6.0, ((0, 64), (1, 8)))
    cotangent = scatter_about(streams_of[1], (TOKENS, D), 1.0, 6.0, ((0, 64), (1, 8)))
    expert_ids_keys = jax.random.split(jax.random.fold_in(streams_of[2], 1), TOKENS // TOK_DEV)
    expert_ids_turns = jax.random.permutation(jax.random.fold_in(streams_of[2], 3), TOKENS // TOK_DEV)
    expert_ids = jax.vmap(lambda own, number: assign_block(jax.random.fold_in(streams_of[2], 2), own, number, TOK_DEV, EXPERTS, TOP, CAP, 2))(expert_ids_keys, expert_ids_turns).reshape((TOKENS, TOP))
    gate_values = jnp.clip(0.1 + 0.9 * jax.random.uniform(streams_of[3], (TOKENS, TOP), jnp.float32) ** block_levels(streams_of[3], (TOKENS, TOP), ((0, 64),), -0.2, 0.2), 0.1, 1.0)
    w_gate = scatter_about(streams_of[4], (EXPERTS, FF, D), D ** -0.5, 0.125, ((0, 64), (1, 8)))
    w_up = scatter_about(streams_of[5], (EXPERTS, FF, D), D ** -0.5, 0.125, ((0, 64), (1, 8)))
    w_down = scatter_about(streams_of[6], (EXPERTS, FF, D), FF ** -0.5, 0.15625, ((0, 64), (1, 8)))
    return dict(tokens=tokens, cotangent=cotangent, expert_ids=expert_ids, gate_values=gate_values, w_gate=w_gate, w_up=w_up, w_down=w_down)


def slot_numbers(flat_ids, experts):
    onehot = (flat_ids[:, None] == jnp.arange(experts, dtype=jnp.int32)[None, :]).astype(jnp.int32)
    before = jnp.cumsum(onehot, axis=0) - onehot
    return jnp.sum(before * onehot, axis=1).astype(jnp.int32)


def pair_table(expert_ids, experts, capacity):
    flat_ids = expert_ids.reshape(-1).astype(jnp.int32)
    position = (flat_ids * capacity + slot_numbers(flat_ids, experts)).astype(jnp.int32)
    matches = position[None, :] == jnp.arange(experts * capacity, dtype=jnp.int32)[:, None]
    usable = jnp.any(matches, axis=1)
    numbers = jnp.arange(flat_ids.shape[0], dtype=jnp.int32)[None, :]
    pair_index = jnp.sum(jnp.where(matches, numbers, 0), axis=1).astype(jnp.int32)
    return pair_index, usable, position


def dispatch_rows(features, cotangent, gate_values, pair_index, usable, top_count):
    token_index = (pair_index // top_count).astype(jnp.int32)
    feature_rows = jnp.where(usable[:, None], features[token_index], jnp.zeros((), features.dtype))
    scaled = gate_values.reshape(-1)[pair_index][:, None] * cotangent[token_index].astype(jnp.float32)
    cotangent_rows = jnp.where(usable[:, None], scaled, jnp.zeros((), jnp.float32)).astype(jnp.bfloat16)
    return feature_rows, cotangent_rows


def one_expert(inputs):
    expert_inputs, expert_cotangent, gate_weight, up_weight, down_weight = inputs
    row_count = expert_inputs.shape[0]
    gate_pre = jnp.dot(expert_inputs, gate_weight.T, preferred_element_type=jnp.float32)
    up_proj = jnp.dot(expert_inputs, up_weight.T, preferred_element_type=jnp.float32)
    sigmoid_gate = jax.nn.sigmoid(gate_pre)
    swish_value = gate_pre * sigmoid_gate
    hidden = (swish_value * up_proj).astype(jnp.bfloat16)
    hidden_grad = jnp.dot(expert_cotangent, down_weight.T, preferred_element_type=jnp.float32)
    gate_grad = (hidden_grad * up_proj * sigmoid_gate * (1.0 + gate_pre * (1.0 - sigmoid_gate))).astype(jnp.bfloat16)
    up_grad = (hidden_grad * swish_value).astype(jnp.bfloat16)
    grad_gate = jnp.dot(gate_grad.T, expert_inputs, preferred_element_type=jnp.float32).astype(jnp.bfloat16)
    grad_up = jnp.dot(up_grad.T, expert_inputs, preferred_element_type=jnp.float32).astype(jnp.bfloat16)
    grad_down = jnp.dot(hidden.T, expert_cotangent, preferred_element_type=jnp.float32).astype(jnp.bfloat16)
    slice_units = FF // N_TP
    gate_slices = gate_grad.astype(jnp.float32).reshape(row_count, N_TP, slice_units)
    up_slices = up_grad.astype(jnp.float32).reshape(row_count, N_TP, slice_units)
    gate_blocks = gate_weight.astype(jnp.float32).reshape(N_TP, slice_units, D)
    up_blocks = up_weight.astype(jnp.float32).reshape(N_TP, slice_units, D)
    terms = jnp.einsum("rtf,tfd->trd", gate_slices, gate_blocks, precision=lax.Precision.HIGHEST)
    terms = terms + jnp.einsum("rtf,tfd->trd", up_slices, up_blocks, precision=lax.Precision.HIGHEST)
    rounded = lax.optimization_barrier(terms.astype(jnp.bfloat16))
    input_rows = jnp.sum(rounded.astype(jnp.float32), axis=0).astype(jnp.bfloat16)
    return grad_gate, grad_up, grad_down, input_rows


def combine_rows(returned, position):
    picked = returned[position].astype(jnp.float32)
    return jnp.sum(picked.reshape(TOK_DEV, TOP, D), axis=1).astype(jnp.bfloat16)


def reference(tokens, cotangent, expert_ids, gate_values, w_gate, w_up, w_down):
    experts = N_EP
    pair_index, usable, position = jax.vmap(partial(pair_table, experts=experts, capacity=CAP))(expert_ids.reshape(N_EP, TOK_DEV, TOP))
    feature_rows, cotangent_rows = jax.vmap(partial(dispatch_rows, top_count=TOP))(
        tokens.reshape(N_EP, TOK_DEV, D), cotangent.reshape(N_EP, TOK_DEV, D),
        gate_values.reshape(N_EP, TOK_DEV, TOP), pair_index, usable)
    feature_rows = jnp.swapaxes(feature_rows.reshape(N_EP, experts, CAP, D), 0, 1).reshape(experts, N_EP * CAP, D)
    cotangent_rows = jnp.swapaxes(cotangent_rows.reshape(N_EP, experts, CAP, D), 0, 1).reshape(experts, N_EP * CAP, D)
    grad_gate, grad_up, grad_down, input_rows = lax.map(one_expert, (feature_rows, cotangent_rows, w_gate, w_up, w_down))
    returned = jnp.swapaxes(input_rows.reshape(experts, N_EP, CAP, D), 0, 1).reshape(N_EP, experts * CAP, D)
    input_grad = jax.vmap(combine_rows)(returned, position).reshape(TOKENS, D)
    return input_grad, grad_gate, grad_up, grad_down
```

```python
import jax
import jax.numpy as jnp
import numpy as np
from jax import lax
from jax.experimental import pallas as pl
from jax.experimental.pallas import tpu as pltpu
from jax.sharding import PartitionSpec as P

VMEM = pl.BlockSpec(memory_space=pltpu.VMEM)
SMEM = pl.BlockSpec(memory_space=pltpu.SMEM)
PARAMS = pltpu.CompilerParams(vmem_limit_bytes=48 * 1024 * 1024)


def nt(left, right):
    return lax.dot_general(left, right, (((1,), (1,)), ((), ())), preferred_element_type=jnp.float32)


def tn(left, right):
    return lax.dot_general(left, right, (((0,), (0,)), ((), ())), preferred_element_type=jnp.float32)


def nn(left, right):
    return jnp.dot(left, right, preferred_element_type=jnp.float32)


def dispatch(ids, gates, both, experts, slots):
    top, tokens = ids.shape
    width = both.shape[1] // 2
    count = experts * slots

    def kernel(ids_ref, gates_ref, both_ref, rows_ref, place_ref):
        ids = ids_ref[...]
        gates = gates_ref[...]
        expert = lax.broadcasted_iota(jnp.int32, (experts, tokens), 0)
        named = jnp.zeros((experts, tokens), jnp.float32)
        gate = jnp.zeros((experts, tokens), jnp.float32)
        for k in range(top):
            hit = ids[k : k + 1, :] == expert
            named = jnp.where(hit, 1.0, named)
            gate = jnp.where(hit, gates[k : k + 1, :], gate)
        earlier = (
            lax.broadcasted_iota(jnp.int32, (tokens, tokens), 0)
            < lax.broadcasted_iota(jnp.int32, (tokens, tokens), 1)
        ).astype(jnp.float32)
        before = nn(named.astype(jnp.bfloat16), earlier.astype(jnp.bfloat16))
        slot = jnp.where(named > 0.0, before, -1.0)
        shape = (experts, slots, tokens)
        wanted = lax.broadcasted_iota(jnp.int32, shape, 1).astype(jnp.float32)
        match = jnp.broadcast_to(slot[:, None, :], shape) == wanted
        scale = jnp.where(match, jnp.broadcast_to(gate[:, None, :], shape), 0.0)
        scale = jnp.sum(scale.reshape(count, tokens), axis=1, keepdims=True)
        place = match.astype(jnp.float32).reshape(count, tokens).astype(jnp.bfloat16)
        place_ref[...] = place
        rows_ref[:, :width] = nn(place, both_ref[:, :width]).astype(jnp.bfloat16)
        rows_ref[:, width:] = (scale * nn(place, both_ref[:, width:])).astype(jnp.bfloat16)

    return pl.pallas_call(
        kernel,
        out_shape=(
            jax.ShapeDtypeStruct((count, 2 * width), jnp.bfloat16),
            jax.ShapeDtypeStruct((count, tokens), jnp.bfloat16),
        ),
        in_specs=[VMEM] * 3,
        out_specs=(VMEM, VMEM),
        compiler_params=PARAMS,
        name="dispatch",
    )(ids, gates, both)


def first_products(owners, features, cotangents, weights):
    count = len(features)
    rows, width = features[0].shape
    units = weights[0].shape[0]

    def kernel(owners_ref, *refs):
        x, g = refs[:count], refs[count : 2 * count]
        w_gate, w_up, w_down = refs[2 * count : 2 * count + 3]
        a_ref, b_ref, dh_ref = refs[2 * count + 3 :]
        for k in range(count):
            part = pl.ds(pl.multiple_of(owners_ref[k] * width, width), width)
            a, b = nt(w_gate[:, part], x[k][...]), nt(w_up[:, part], x[k][...])
            dh = nt(w_down[:, part], g[k][...])
            if k == 0:
                a_ref[...], b_ref[...], dh_ref[...] = a, b, dh
            else:
                a_ref[...] += a
                b_ref[...] += b
                dh_ref[...] += dh

    return pl.pallas_call(
        kernel,
        out_shape=[jax.ShapeDtypeStruct((units, rows), jnp.float32)] * 3,
        in_specs=[SMEM] + [VMEM] * (2 * count + 3),
        out_specs=[VMEM] * 3,
        compiler_params=PARAMS,
        name="first_products",
    )(owners, *features, *cotangents, *weights)


def activations(owners, features, cotangents, weights, sums):
    count = len(features)
    rows, width = features[0].shape
    units = weights[0].shape[0]

    def kernel(owners_ref, *refs):
        x, g = refs[:count], refs[count : 2 * count]
        w_gate, w_up, w_down = refs[2 * count : 2 * count + 3]
        a_ref, b_ref, dh_ref = refs[2 * count + 3 : 2 * count + 6]
        grads_ref, hidden_ref = refs[2 * count + 6 :]
        a, b, dh = a_ref[...], b_ref[...], dh_ref[...]
        for k in range(count):
            part = pl.ds(pl.multiple_of(owners_ref[k] * width, width), width)
            a += nt(w_gate[:, part], x[k][...])
            b += nt(w_up[:, part], x[k][...])
            dh += nt(w_down[:, part], g[k][...])
        s = jax.nn.sigmoid(a)
        swish = a * s
        hidden_ref[...] = (swish * b).astype(jnp.bfloat16)
        grads_ref[:units, :] = (dh * b * s * (1.0 + a * (1.0 - s))).astype(jnp.bfloat16)
        grads_ref[units:, :] = (dh * swish).astype(jnp.bfloat16)

    return pl.pallas_call(
        kernel,
        out_shape=(
            jax.ShapeDtypeStruct((2 * units, rows), jnp.bfloat16),
            jax.ShapeDtypeStruct((units, rows), jnp.bfloat16),
        ),
        in_specs=[SMEM] + [VMEM] * (2 * count + 6),
        out_specs=(VMEM, VMEM),
        compiler_params=PARAMS,
        name="activations",
    )(owners, *features, *cotangents, *weights, *sums)


def weight_grads(owners, features, cotangents, grads, hidden):
    count = len(features)
    rows, width = features[0].shape
    units = hidden.shape[0]

    def kernel(owners_ref, *refs):
        x, g = refs[:count], refs[count : 2 * count]
        grads_ref, hidden_ref, gate_ref, up_ref, down_ref = refs[2 * count :]
        for k in range(count):
            part = pl.ds(pl.multiple_of(owners_ref[k] * width, width), width)
            both = nn(grads_ref[...], x[k][...]).astype(jnp.bfloat16)
            gate_ref[:, part] = both[:units]
            up_ref[:, part] = both[units:]
            down_ref[:, part] = nn(hidden_ref[...], g[k][...]).astype(jnp.bfloat16)

    return pl.pallas_call(
        kernel,
        out_shape=[jax.ShapeDtypeStruct((units, count * width), jnp.bfloat16)] * 3,
        in_specs=[SMEM] + [VMEM] * (2 * count + 2),
        out_specs=[VMEM] * 3,
        compiler_params=PARAMS,
        name="weight_grads",
    )(owners, *features, *cotangents, grads, hidden)


def local(tokens, cotangent, expert_ids, gate_values, w_gate, w_up, w_down):
    groups = lax.axis_size("ep")
    ring = lax.axis_size("tp")
    half = ring // 2
    tok_count, top_count = expert_ids.shape
    slots = max(2, tok_count * top_count * 4 // (groups * 3))
    width = tokens.shape[1]
    rows = groups * slots
    me = lax.axis_index("tp")
    weights = (w_gate[0], w_up[0], w_down[0])

    def moved(value, by):
        return lax.ppermute(value, "tp", [(i, (i + by) % ring) for i in range(ring)])

    def over_ep(value):
        shape = (groups, slots, value.shape[1])
        value = lax.all_to_all(value.reshape(shape), "ep", split_axis=0, concat_axis=0, tiled=True)
        return value.reshape(rows, -1)

    ids, gates = expert_ids.T, gate_values.T
    both = jnp.concatenate([tokens, cotangent], axis=1)
    far_both = moved(both, half)
    sent, place = dispatch(ids, gates, both, groups, slots)
    mine = over_ep(sent)
    far_sent, _ = dispatch(ids, gates, far_both, groups, slots)
    mine, far_sent = lax.optimization_barrier((mine, far_sent))
    far = over_ep(far_sent)

    x, g = {0: mine[:, :width]}, {0: mine[:, width:]}
    x[half], g[half] = far[:, :width], far[:, width:]
    for step in range(1, half):
        for blocks in (x, g):
            blocks[-step] = moved(blocks[1 - step], 1)
            blocks[step] = moved(blocks[step - 1], -1)

    def owners(order):
        steps = np.array([d % ring for d in order], np.int32)
        return lax.rem(me.astype(jnp.int32) + steps, np.int32(ring))

    def picked(blocks, order):
        return [blocks[d] for d in order]

    early = [d for step in range(half - 1) for d in ([-step, step] if step else [0])]
    late = [1 - half, half - 1, half]
    sums = first_products(owners(early), picked(x, early), picked(g, early), weights)
    grads, hidden = activations(owners(late), picked(x, late), picked(g, late), weights, sums)

    paired = jnp.concatenate(weights[:2], axis=0)

    def partial(d):
        at = lax.rem(me + d % ring, ring) * width
        return tn(grads, lax.dynamic_slice_in_dim(paired, at, width, axis=1))

    far_back = over_ep(partial(half).astype(jnp.bfloat16))
    right = partial(half - 1).astype(jnp.bfloat16)
    left = partial(1 - half).astype(jnp.bfloat16)
    for d in range(half - 2, -1, -1):
        right, left = moved(right, 1), moved(left, -1)
        if d:
            right = (right.astype(jnp.float32) + partial(d)).astype(jnp.bfloat16)
            left = (left.astype(jnp.float32) + partial(-d)).astype(jnp.bfloat16)
    total = partial(0) + right.astype(jnp.float32) + left.astype(jnp.float32)

    order = early + late
    grad_gate, grad_up, grad_down = weight_grads(
        owners(order), picked(x, order), picked(g, order), grads, hidden
    )
    back = over_ep(total.astype(jnp.bfloat16))
    far_tokens = moved(tn(place, far_back).astype(jnp.bfloat16), half)
    input_grad = (tn(place, back) + far_tokens.astype(jnp.float32)).astype(jnp.bfloat16)
    return (input_grad, grad_gate[None], grad_up[None], grad_down[None])


def solution(mesh):
    in_specs = (
        P("ep", "tp"),
        P("ep", "tp"),
        P("ep", None),
        P("ep", None),
        P("ep", "tp", None),
        P("ep", "tp", None),
        P("ep", "tp", None),
    )
    out_specs = (P("ep", "tp"), P("ep", "tp", None), P("ep", "tp", None), P("ep", "tp", None))
    return jax.shard_map(local, mesh=mesh, in_specs=in_specs, out_specs=out_specs, check_vma=False)
```

```python
import jax
import jax.numpy as jnp
import numpy as np
from jax import lax
from jax.experimental import pallas as pl
from jax.experimental.pallas import tpu as pltpu
from jax.sharding import PartitionSpec as P

VMEM = pl.BlockSpec(memory_space=pltpu.VMEM)
SMEM = pl.BlockSpec(memory_space=pltpu.SMEM)
PARAMS = pltpu.CompilerParams(vmem_limit_bytes=48 * 1024 * 1024)


def nt(left, right):
    return lax.dot_general(left, right, (((1,), (1,)), ((), ())), preferred_element_type=jnp.float32)


def tn(left, right):
    return lax.dot_general(left, right, (((0,), (0,)), ((), ())), preferred_element_type=jnp.float32)


def nn(left, right):
    return jnp.dot(left, right, preferred_element_type=jnp.float32)


def dispatch(ids, gates, pieces, experts, slots):
    top, tokens = ids.shape
    count = experts * slots
    widths = [piece.shape[1] for piece, _ in pieces]
    scaled = [flag for _, flag in pieces]

    def kernel(ids_ref, gates_ref, *refs):
        rows_ref, place_ref = refs[-2:]
        ids = ids_ref[...]
        gates = gates_ref[...]
        expert = lax.broadcasted_iota(jnp.int32, (experts, tokens), 0)
        named = jnp.zeros((experts, tokens), jnp.float32)
        gate = jnp.zeros((experts, tokens), jnp.float32)
        for k in range(top):
            hit = ids[k : k + 1, :] == expert
            named = jnp.where(hit, 1.0, named)
            gate = jnp.where(hit, gates[k : k + 1, :], gate)
        earlier = (
            lax.broadcasted_iota(jnp.int32, (tokens, tokens), 0)
            < lax.broadcasted_iota(jnp.int32, (tokens, tokens), 1)
        ).astype(jnp.float32)
        before = nn(named.astype(jnp.bfloat16), earlier.astype(jnp.bfloat16))
        slot = jnp.where(named > 0.0, before, -1.0)
        shape = (experts, slots, tokens)
        wanted = lax.broadcasted_iota(jnp.int32, shape, 1).astype(jnp.float32)
        match = jnp.broadcast_to(slot[:, None, :], shape) == wanted
        scale = jnp.where(match, jnp.broadcast_to(gate[:, None, :], shape), 0.0)
        scale = jnp.sum(scale.reshape(count, tokens), axis=1, keepdims=True)
        place = match.astype(jnp.float32).reshape(count, tokens).astype(jnp.bfloat16)
        place_ref[...] = place
        at = 0
        for k, ref in enumerate(refs[:-2]):
            rows = nn(place, ref[...])
            if scaled[k]:
                rows = scale * rows
            rows_ref[:, at : at + widths[k]] = rows.astype(jnp.bfloat16)
            at += widths[k]

    return pl.pallas_call(
        kernel,
        out_shape=(
            jax.ShapeDtypeStruct((count, sum(widths)), jnp.bfloat16),
            jax.ShapeDtypeStruct((count, tokens), jnp.bfloat16),
        ),
        in_specs=[VMEM] * (2 + len(pieces)),
        out_specs=(VMEM, VMEM),
        compiler_params=PARAMS,
        name="dispatch",
    )(ids, gates, *[piece for piece, _ in pieces])


def gathered(terms):
    arrays, table = [], []
    for array, column, owner in terms:
        known = [k for k, other in enumerate(arrays) if other is array]
        if not known:
            arrays.append(array)
        table.append((known[0] if known else len(arrays) - 1, column, owner))
    return arrays, table


def first_products(me, ring, width, features, cotangents, weights):
    arrays, table = gathered(features + cotangents)
    rows = arrays[0].shape[0]
    units = weights[0].shape[0]

    def kernel(me_ref, *refs):
        w_gate, w_up, w_down, a_ref, b_ref, dh_ref = refs[len(arrays) :]
        for k, (number, column, owner) in enumerate(table):
            block = refs[number][:, column : column + width]
            start = lax.rem(me_ref[0] + owner % ring, ring) * width
            part = pl.ds(pl.multiple_of(start, width), width)
            if k == 0:
                a_ref[...], b_ref[...] = nt(w_gate[:, part], block), nt(w_up[:, part], block)
            elif k < len(features):
                a_ref[...] += nt(w_gate[:, part], block)
                b_ref[...] += nt(w_up[:, part], block)
            elif k == len(features):
                dh_ref[...] = nt(w_down[:, part], block)
            else:
                dh_ref[...] += nt(w_down[:, part], block)

    return pl.pallas_call(
        kernel,
        out_shape=[jax.ShapeDtypeStruct((units, rows), jnp.float32)] * 3,
        in_specs=[SMEM] + [VMEM] * (len(arrays) + 3),
        out_specs=[VMEM] * 3,
        compiler_params=PARAMS,
        name="first_products",
    )(me, *arrays, *weights)


def activations(me, ring, width, features, cotangents, weights, sums):
    arrays, table = gathered(features + cotangents)
    rows = arrays[0].shape[0]
    units = weights[0].shape[0]

    def kernel(me_ref, *refs):
        w_gate, w_up, w_down, a_ref, b_ref, dh_ref, grads_ref, hidden_ref = refs[len(arrays) :]
        a, b, dh = a_ref[...], b_ref[...], dh_ref[...]
        for k, (number, column, owner) in enumerate(table):
            block = refs[number][:, column : column + width]
            start = lax.rem(me_ref[0] + owner % ring, ring) * width
            part = pl.ds(pl.multiple_of(start, width), width)
            if k < len(features):
                a += nt(w_gate[:, part], block)
                b += nt(w_up[:, part], block)
            else:
                dh += nt(w_down[:, part], block)
        s = jax.nn.sigmoid(a)
        swish = a * s
        hidden_ref[...] = (swish * b).astype(jnp.bfloat16)
        grads_ref[:units, :] = (dh * b * s * (1.0 + a * (1.0 - s))).astype(jnp.bfloat16)
        grads_ref[units:, :] = (dh * swish).astype(jnp.bfloat16)

    return pl.pallas_call(
        kernel,
        out_shape=(
            jax.ShapeDtypeStruct((2 * units, rows), jnp.bfloat16),
            jax.ShapeDtypeStruct((units, rows), jnp.bfloat16),
        ),
        in_specs=[SMEM] + [VMEM] * (len(arrays) + 6),
        out_specs=(VMEM, VMEM),
        compiler_params=PARAMS,
        name="activations",
    )(me, *arrays, *weights, *sums)


def weight_grads(me, ring, width, features, cotangents, grads, hidden):
    arrays, table = gathered(features + cotangents)
    units = hidden.shape[0]

    def kernel(me_ref, *refs):
        grads_ref, hidden_ref, gate_ref, up_ref, down_ref = refs[len(arrays) :]
        for k, (number, column, owner) in enumerate(table):
            block = refs[number][:, column : column + width]
            start = lax.rem(me_ref[0] + owner % ring, ring) * width
            part = pl.ds(pl.multiple_of(start, width), width)
            if k < len(features):
                both = nn(grads_ref[...], block).astype(jnp.bfloat16)
                gate_ref[:, part] = both[:units]
                up_ref[:, part] = both[units:]
            else:
                down_ref[:, part] = nn(hidden_ref[...], block).astype(jnp.bfloat16)

    return pl.pallas_call(
        kernel,
        out_shape=[jax.ShapeDtypeStruct((units, ring * width), jnp.bfloat16)] * 3,
        in_specs=[SMEM] + [VMEM] * (len(arrays) + 2),
        out_specs=[VMEM] * 3,
        compiler_params=PARAMS,
        name="weight_grads",
    )(me, *arrays, grads, hidden)


def local(tokens, cotangent, expert_ids, gate_values, w_gate, w_up, w_down):
    groups = lax.axis_size("ep")
    ring = lax.axis_size("tp")
    half = ring // 2
    near = half - 1
    tok_count, top_count = expert_ids.shape
    slots = max(2, tok_count * top_count * 4 // (groups * 3))
    width = tokens.shape[1]
    rows = groups * slots
    me = lax.axis_index("tp").astype(jnp.int32)
    me_ref = me.reshape(1)
    weights = (w_gate[0], w_up[0], w_down[0])

    def moved(value, by):
        return lax.ppermute(value, "tp", [(i, (i + by) % ring) for i in range(ring)])

    def over_ep(value):
        shape = (groups, slots, value.shape[1])
        value = lax.all_to_all(value.reshape(shape), "ep", split_axis=0, concat_axis=0, tiled=True)
        return value.reshape(rows, -1)

    ids, gates = expert_ids.T, gate_values.T
    sent, place = dispatch(ids, gates, [(tokens, False), (cotangent, True)], groups, slots)
    far_tokens, far_cot, sent = lax.optimization_barrier((tokens, cotangent, sent))
    mine = over_ep(sent)
    far_both = moved(jnp.concatenate([far_tokens, far_cot], axis=1), half)
    side_tokens = moved(far_tokens, -near)
    side_cot = moved(far_cot, near)
    far_sent, _ = dispatch(
        ids,
        gates,
        [
            (far_both[:, :width], False),
            (far_both[:, width:], True),
            (side_tokens, False),
            (side_cot, True),
        ],
        groups,
        slots,
    )
    x0, g0 = mine[:, :width], mine[:, width:]
    x0, g0, far_sent = lax.optimization_barrier((x0, g0, far_sent))
    x, g = {0: x0}, {0: g0}
    for step in range(1, near):
        for blocks in (x, g):
            blocks[-step] = moved(blocks[1 - step], 1)
            blocks[step] = moved(blocks[step - 1], -1)
    x[-near] = moved(x[1 - near], 1)
    g[near] = moved(g[near - 1], -1)
    far = over_ep(far_sent)

    early = [d for step in range(near) for d in ([-step, step] if step else [0])]
    early_x, early_g = [(x[d], 0, d) for d in early], [(g[d], 0, d) for d in early]
    late_x = [(far, 0, half), (far, 2 * width, near), (x[-near], 0, -near)]
    late_g = [(far, width, half), (far, 3 * width, -near), (g[near], 0, near)]
    sums = first_products(me_ref, ring, width, early_x, early_g, weights)
    grads, hidden = activations(me_ref, ring, width, late_x, late_g, weights, sums)

    paired = jnp.concatenate(weights[:2], axis=0)

    def columns(d):
        start = lax.rem(me + d % ring, np.int32(ring)) * width
        return lax.dynamic_slice_in_dim(paired, start, width, axis=1)

    def partial(d):
        return lax.optimization_barrier(tn(grads, columns(d)).astype(jnp.bfloat16))

    def added(*values):
        return sum(value.astype(jnp.float32) for value in values)

    away = [half, near, -near]
    right, left = partial(near - 1), partial(1 - near)
    side = jnp.concatenate([columns(d) for d in away], axis=1)
    far_back = over_ep(tn(grads, side).astype(jnp.bfloat16))
    for d in range(near - 2, -1, -1):
        right, left = moved(right, 1), moved(left, -1)
        if d:
            right = added(right, partial(d)).astype(jnp.bfloat16)
            left = added(left, partial(-d)).astype(jnp.bfloat16)
    back = over_ep(added(partial(0), right, left).astype(jnp.bfloat16))

    grad_gate, grad_up, grad_down = weight_grads(
        me_ref, ring, width, early_x + late_x, early_g + late_g, grads, hidden
    )
    sides = tn(place, far_back).astype(jnp.bfloat16)
    sides = [moved(sides[:, k * width : (k + 1) * width], d) for k, d in enumerate(away)]
    input_grad = (tn(place, back) + added(*sides)).astype(jnp.bfloat16)
    return (input_grad, grad_gate[None], grad_up[None], grad_down[None])


def solution(mesh):
    in_specs = (
        P("ep", "tp"),
        P("ep", "tp"),
        P("ep", None),
        P("ep", None),
        P("ep", "tp", None),
        P("ep", "tp", None),
        P("ep", "tp", None),
    )
    out_specs = (P("ep", "tp"), P("ep", "tp", None), P("ep", "tp", None), P("ep", "tp", None))
    return jax.shard_map(local, mesh=mesh, in_specs=in_specs, out_specs=out_specs, check_vma=False)
```

```python
import jax
import jax.numpy as jnp
import numpy as np
from jax import lax
from jax.experimental import pallas as pl
from jax.experimental.pallas import tpu as pltpu
from jax.sharding import PartitionSpec as P

VMEM = pl.BlockSpec(memory_space=pltpu.VMEM)
SMEM = pl.BlockSpec(memory_space=pltpu.SMEM)
PARAMS = pltpu.CompilerParams(vmem_limit_bytes=56 * 1024 * 1024)


def nt(left, right):
    return lax.dot_general(left, right, (((1,), (1,)), ((), ())), preferred_element_type=jnp.float32)


def tn(left, right):
    return lax.dot_general(left, right, (((0,), (0,)), ((), ())), preferred_element_type=jnp.float32)


def nn(left, right):
    return jnp.dot(left, right, preferred_element_type=jnp.float32)


def dispatch(ids, gates, pieces, experts, slots):
    top, tokens = ids.shape
    count = experts * slots
    widths = [piece.shape[1] for piece, _ in pieces]
    scaled = [flag for _, flag in pieces]

    def kernel(ids_ref, gates_ref, *refs):
        rows_ref, place_ref = refs[-2:]
        ids = ids_ref[...]
        gates = gates_ref[...]
        expert = lax.broadcasted_iota(jnp.int32, (experts, tokens), 0)
        named = jnp.zeros((experts, tokens), jnp.float32)
        gate = jnp.zeros((experts, tokens), jnp.float32)
        for k in range(top):
            hit = ids[k : k + 1, :] == expert
            named = jnp.where(hit, 1.0, named)
            gate = jnp.where(hit, gates[k : k + 1, :], gate)
        earlier = (
            lax.broadcasted_iota(jnp.int32, (tokens, tokens), 0)
            < lax.broadcasted_iota(jnp.int32, (tokens, tokens), 1)
        ).astype(jnp.float32)
        before = nn(named.astype(jnp.bfloat16), earlier.astype(jnp.bfloat16))
        slot = jnp.where(named > 0.0, before, -1.0)
        shape = (experts, slots, tokens)
        wanted = lax.broadcasted_iota(jnp.int32, shape, 1).astype(jnp.float32)
        match = jnp.broadcast_to(slot[:, None, :], shape) == wanted
        scale = jnp.where(match, jnp.broadcast_to(gate[:, None, :], shape), 0.0)
        scale = jnp.sum(scale.reshape(count, tokens), axis=1, keepdims=True)
        place = match.astype(jnp.float32).reshape(count, tokens).astype(jnp.bfloat16)
        place_ref[...] = place
        at = 0
        for k, ref in enumerate(refs[:-2]):
            rows = nn(place, ref[...])
            if scaled[k]:
                rows = scale * rows
            rows_ref[:, at : at + widths[k]] = rows.astype(jnp.bfloat16)
            at += widths[k]

    return pl.pallas_call(
        kernel,
        out_shape=(
            jax.ShapeDtypeStruct((count, sum(widths)), jnp.bfloat16),
            jax.ShapeDtypeStruct((count, tokens), jnp.bfloat16),
        ),
        in_specs=[VMEM] * (2 + len(pieces)),
        out_specs=(VMEM, VMEM),
        compiler_params=PARAMS,
        name="dispatch",
    )(ids, gates, *[piece for piece, _ in pieces])


def gathered(terms):
    arrays, table = [], []
    for array, column, owner in terms:
        known = [k for k, other in enumerate(arrays) if other is array]
        if not known:
            arrays.append(array)
        table.append((known[0] if known else len(arrays) - 1, column, owner))
    return arrays, table


def first_products(me, ring, width, features, cotangents, weights):
    arrays, table = gathered(features + cotangents)
    rows = arrays[0].shape[0]
    units = weights[0].shape[0]

    def kernel(me_ref, *refs):
        w_gate, w_up, w_down, a_ref, b_ref, dh_ref = refs[len(arrays) :]
        for k, (number, column, owner) in enumerate(table):
            block = refs[number][:, column : column + width]
            start = lax.rem(me_ref[0] + owner % ring, ring) * width
            part = pl.ds(pl.multiple_of(start, width), width)
            if k == 0:
                a_ref[...], b_ref[...] = nt(w_gate[:, part], block), nt(w_up[:, part], block)
            elif k < len(features):
                a_ref[...] += nt(w_gate[:, part], block)
                b_ref[...] += nt(w_up[:, part], block)
            elif k == len(features):
                dh_ref[...] = nt(w_down[:, part], block)
            else:
                dh_ref[...] += nt(w_down[:, part], block)

    return pl.pallas_call(
        kernel,
        out_shape=[jax.ShapeDtypeStruct((units, rows), jnp.float32)] * 3,
        in_specs=[SMEM] + [VMEM] * (len(arrays) + 3),
        out_specs=[VMEM] * 3,
        compiler_params=PARAMS,
        cost_estimate=pl.CostEstimate(flops=36 * 10**9, bytes_accessed=1000, transcendentals=0),
        name="first_products",
    )(me, *arrays, *weights)


def activations(me, ring, width, features, cotangents, weights, sums):
    arrays, table = gathered(features + cotangents)
    rows = arrays[0].shape[0]
    units = weights[0].shape[0]

    def kernel(me_ref, *refs):
        w_gate, w_up, w_down, a_ref, b_ref, dh_ref, grads_ref, hidden_ref = refs[len(arrays) :]
        a, b, dh = a_ref[...], b_ref[...], dh_ref[...]
        for k, (number, column, owner) in enumerate(table):
            block = refs[number][:, column : column + width]
            start = lax.rem(me_ref[0] + owner % ring, ring) * width
            part = pl.ds(pl.multiple_of(start, width), width)
            if k < len(features):
                a += nt(w_gate[:, part], block)
                b += nt(w_up[:, part], block)
            else:
                dh += nt(w_down[:, part], block)
        s = jax.nn.sigmoid(a)
        swish = a * s
        hidden_ref[...] = (swish * b).astype(jnp.bfloat16)
        grads_ref[:units, :] = (dh * b * s * (1.0 + a * (1.0 - s))).astype(jnp.bfloat16)
        grads_ref[units:, :] = (dh * swish).astype(jnp.bfloat16)

    return pl.pallas_call(
        kernel,
        out_shape=(
            jax.ShapeDtypeStruct((2 * units, rows), jnp.bfloat16),
            jax.ShapeDtypeStruct((units, rows), jnp.bfloat16),
        ),
        in_specs=[SMEM] + [VMEM] * (len(arrays) + 6),
        out_specs=(VMEM, VMEM),
        compiler_params=PARAMS,
        name="activations",
    )(me, *arrays, *weights, *sums)


def weight_grads(me, ring, width, features, cotangents, grads, hidden):
    arrays, table = gathered(features + cotangents)
    units = hidden.shape[0]

    def kernel(me_ref, *refs):
        grads_ref, hidden_ref, gate_ref, up_ref, down_ref = refs[len(arrays) :]
        for k, (number, column, owner) in enumerate(table):
            block = refs[number][:, column : column + width]
            start = lax.rem(me_ref[0] + owner % ring, ring) * width
            part = pl.ds(pl.multiple_of(start, width), width)
            if k < len(features):
                both = nn(grads_ref[...], block).astype(jnp.bfloat16)
                gate_ref[:, part] = both[:units]
                up_ref[:, part] = both[units:]
            else:
                down_ref[:, part] = nn(hidden_ref[...], block).astype(jnp.bfloat16)

    return pl.pallas_call(
        kernel,
        out_shape=[jax.ShapeDtypeStruct((units, ring * width), jnp.bfloat16)] * 3,
        in_specs=[SMEM] + [VMEM] * (len(arrays) + 2),
        out_specs=[VMEM] * 3,
        compiler_params=PARAMS,
        cost_estimate=pl.CostEstimate(flops=20 * 10**9, bytes_accessed=1000, transcendentals=0),
        name="weight_grads",
    )(me, *arrays, grads, hidden)


def local(tokens, cotangent, expert_ids, gate_values, w_gate, w_up, w_down):
    groups = lax.axis_size("ep")
    ring = lax.axis_size("tp")
    half = ring // 2
    near = half - 1
    tok_count, top_count = expert_ids.shape
    slots = max(2, tok_count * top_count * 4 // (groups * 3))
    width = tokens.shape[1]
    rows = groups * slots
    me = lax.axis_index("tp").astype(jnp.int32)
    me_ref = me.reshape(1)
    weights = (w_gate[0], w_up[0], w_down[0])

    def moved(value, by):
        return lax.ppermute(value, "tp", [(i, (i + by) % ring) for i in range(ring)])

    def over_ep(value):
        shape = (groups, slots, value.shape[1])
        value = lax.all_to_all(value.reshape(shape), "ep", split_axis=0, concat_axis=0, tiled=True)
        return value.reshape(rows, -1)

    ids, gates = expert_ids.T, gate_values.T
    sent, place = dispatch(ids, gates, [(tokens, False), (cotangent, True)], groups, slots)
    far_tokens, far_cot, sent = lax.optimization_barrier((tokens, cotangent, sent))
    mine = over_ep(sent)
    far_both = moved(jnp.concatenate([far_tokens, far_cot], axis=1), half)
    side_tokens = moved(far_tokens, -near)
    side_cot = moved(far_cot, near)
    far_sent, _ = dispatch(
        ids,
        gates,
        [
            (far_both[:, :width], False),
            (far_both[:, width:], True),
            (side_tokens, False),
            (side_cot, True),
        ],
        groups,
        slots,
    )
    x0, g0 = mine[:, :width], mine[:, width:]
    x0, g0, far_sent = lax.optimization_barrier((x0, g0, far_sent))
    x, g = {0: x0}, {0: g0}
    for step in range(1, near):
        for blocks in (x, g):
            blocks[-step] = moved(blocks[1 - step], 1)
            blocks[step] = moved(blocks[step - 1], -1)
    x[-near] = moved(x[1 - near], 1)
    g[near] = moved(g[near - 1], -1)
    far = over_ep(far_sent)

    early = [d for step in range(near) for d in ([-step, step] if step else [0])]
    early_x, early_g = [(x[d], 0, d) for d in early], [(g[d], 0, d) for d in early]
    late_x = [(far, 0, half), (far, 2 * width, near), (x[-near], 0, -near)]
    late_g = [(far, width, half), (far, 3 * width, -near), (g[near], 0, near)]
    sums = first_products(me_ref, ring, width, early_x, early_g, weights)
    grads, hidden = activations(me_ref, ring, width, late_x, late_g, weights, sums)

    paired = jnp.concatenate(weights[:2], axis=0)

    def columns(d):
        start = lax.rem(me + d % ring, np.int32(ring)) * width
        return lax.dynamic_slice_in_dim(paired, start, width, axis=1)

    def partial(d):
        return lax.optimization_barrier(tn(grads, columns(d)).astype(jnp.bfloat16))

    def added(*values):
        return sum(value.astype(jnp.float32) for value in values)

    away = [half, near, -near]
    right, left = partial(near - 1), partial(1 - near)
    side = jnp.concatenate([columns(d) for d in away], axis=1)
    far_back = over_ep(tn(grads, side).astype(jnp.bfloat16))
    for d in range(near - 2, -1, -1):
        right, left = moved(right, 1), moved(left, -1)
        if d:
            right = added(right, partial(d)).astype(jnp.bfloat16)
            left = added(left, partial(-d)).astype(jnp.bfloat16)
    total = added(partial(0), right, left).astype(jnp.bfloat16)

    grad_gate, grad_up, grad_down = weight_grads(
        me_ref, ring, width, early_x + late_x, early_g + late_g, grads, hidden
    )
    total, grad_gate, grad_up, grad_down = lax.optimization_barrier(
        (total, grad_gate, grad_up, grad_down)
    )
    back = over_ep(total)
    sides = tn(place, far_back).astype(jnp.bfloat16)
    sides = [moved(sides[:, k * width : (k + 1) * width], d) for k, d in enumerate(away)]
    input_grad = (tn(place, back) + added(*sides)).astype(jnp.bfloat16)
    return (input_grad, grad_gate[None], grad_up[None], grad_down[None])


def solution(mesh):
    in_specs = (
        P("ep", "tp"),
        P("ep", "tp"),
        P("ep", None),
        P("ep", None),
        P("ep", "tp", None),
        P("ep", "tp", None),
        P("ep", "tp", None),
    )
    out_specs = (P("ep", "tp"), P("ep", "tp", None), P("ep", "tp", None), P("ep", "tp", None))
    return jax.shard_map(local, mesh=mesh, in_specs=in_specs, out_specs=out_specs, check_vma=False)
```

```python
import jax
import jax.numpy as jnp
import numpy as np
from jax import lax
from jax.experimental import pallas as pl
from jax.experimental.pallas import tpu as pltpu
from jax.sharding import PartitionSpec as P

VMEM = pl.BlockSpec(memory_space=pltpu.VMEM)
SMEM = pl.BlockSpec(memory_space=pltpu.SMEM)
PARAMS = pltpu.CompilerParams(vmem_limit_bytes=56 * 1024 * 1024)


def nt(left, right):
    return lax.dot_general(left, right, (((1,), (1,)), ((), ())), preferred_element_type=jnp.float32)


def tn(left, right):
    return lax.dot_general(left, right, (((0,), (0,)), ((), ())), preferred_element_type=jnp.float32)


def nn(left, right):
    return jnp.dot(left, right, preferred_element_type=jnp.float32)


def dispatch(ids, gates, pieces, experts, slots):
    top, tokens = ids.shape
    count = experts * slots
    widths = [piece.shape[1] for piece, _ in pieces]
    scaled = [flag for _, flag in pieces]

    def kernel(ids_ref, gates_ref, *refs):
        rows_ref, place_ref = refs[-2:]
        ids = ids_ref[...]
        gates = gates_ref[...]
        expert = lax.broadcasted_iota(jnp.int32, (experts, tokens), 0)
        named = jnp.zeros((experts, tokens), jnp.float32)
        gate = jnp.zeros((experts, tokens), jnp.float32)
        for k in range(top):
            hit = ids[k : k + 1, :] == expert
            named = jnp.where(hit, 1.0, named)
            gate = jnp.where(hit, gates[k : k + 1, :], gate)
        earlier = (
            lax.broadcasted_iota(jnp.int32, (tokens, tokens), 0)
            < lax.broadcasted_iota(jnp.int32, (tokens, tokens), 1)
        ).astype(jnp.float32)
        before = nn(named.astype(jnp.bfloat16), earlier.astype(jnp.bfloat16))
        slot = jnp.where(named > 0.0, before, -1.0)
        shape = (experts, slots, tokens)
        wanted = lax.broadcasted_iota(jnp.int32, shape, 1).astype(jnp.float32)
        match = jnp.broadcast_to(slot[:, None, :], shape) == wanted
        scale = jnp.where(match, jnp.broadcast_to(gate[:, None, :], shape), 0.0)
        scale = jnp.sum(scale.reshape(count, tokens), axis=1, keepdims=True)
        place = match.astype(jnp.float32).reshape(count, tokens).astype(jnp.bfloat16)
        place_ref[...] = place
        at = 0
        for k, ref in enumerate(refs[:-2]):
            rows = nn(place, ref[...])
            if scaled[k]:
                rows = scale * rows
            rows_ref[:, at : at + widths[k]] = rows.astype(jnp.bfloat16)
            at += widths[k]

    return pl.pallas_call(
        kernel,
        out_shape=(
            jax.ShapeDtypeStruct((count, sum(widths)), jnp.bfloat16),
            jax.ShapeDtypeStruct((count, tokens), jnp.bfloat16),
        ),
        in_specs=[VMEM] * (2 + len(pieces)),
        out_specs=(VMEM, VMEM),
        compiler_params=PARAMS,
        name="dispatch",
    )(ids, gates, *[piece for piece, _ in pieces])


def gathered(terms):
    arrays, table = [], []
    for array, column, owner in terms:
        known = [k for k, other in enumerate(arrays) if other is array]
        if not known:
            arrays.append(array)
        table.append((known[0] if known else len(arrays) - 1, column, owner))
    return arrays, table


def first_products(me, ring, width, features, cotangents, weights):
    arrays, table = gathered(features + cotangents)
    rows = arrays[0].shape[0]
    units = weights[0].shape[0]

    def kernel(me_ref, *refs):
        w_gate, w_up, w_down, a_ref, b_ref, dh_ref = refs[len(arrays) :]
        for k, (number, column, owner) in enumerate(table):
            block = refs[number][:, column : column + width]
            start = lax.rem(me_ref[0] + owner % ring, ring) * width
            part = pl.ds(pl.multiple_of(start, width), width)
            if k == 0:
                a_ref[...], b_ref[...] = nt(w_gate[:, part], block), nt(w_up[:, part], block)
            elif k < len(features):
                a_ref[...] += nt(w_gate[:, part], block)
                b_ref[...] += nt(w_up[:, part], block)
            elif k == len(features):
                dh_ref[...] = nt(w_down[:, part], block)
            else:
                dh_ref[...] += nt(w_down[:, part], block)

    return pl.pallas_call(
        kernel,
        out_shape=[jax.ShapeDtypeStruct((units, rows), jnp.float32)] * 3,
        in_specs=[SMEM] + [VMEM] * (len(arrays) + 3),
        out_specs=[VMEM] * 3,
        compiler_params=PARAMS,
        cost_estimate=pl.CostEstimate(flops=3400 * 10**7, bytes_accessed=1000, transcendentals=0),
        name="first_products",
    )(me, *arrays, *weights)


def activations(me, ring, width, features, cotangents, weights, sums):
    arrays, table = gathered(features + cotangents)
    rows = arrays[0].shape[0]
    units = weights[0].shape[0]

    def kernel(me_ref, *refs):
        w_gate, w_up, w_down, a_ref, b_ref, dh_ref, grads_ref, hidden_ref = refs[len(arrays) :]
        a, b, dh = a_ref[...], b_ref[...], dh_ref[...]
        for k, (number, column, owner) in enumerate(table):
            block = refs[number][:, column : column + width]
            start = lax.rem(me_ref[0] + owner % ring, ring) * width
            part = pl.ds(pl.multiple_of(start, width), width)
            if k < len(features):
                a += nt(w_gate[:, part], block)
                b += nt(w_up[:, part], block)
            else:
                dh += nt(w_down[:, part], block)
        s = jax.nn.sigmoid(a)
        swish = a * s
        hidden_ref[...] = (swish * b).astype(jnp.bfloat16)
        grads_ref[:units, :] = (dh * b * s * (1.0 + a * (1.0 - s))).astype(jnp.bfloat16)
        grads_ref[units:, :] = (dh * swish).astype(jnp.bfloat16)

    return pl.pallas_call(
        kernel,
        out_shape=(
            jax.ShapeDtypeStruct((2 * units, rows), jnp.bfloat16),
            jax.ShapeDtypeStruct((units, rows), jnp.bfloat16),
        ),
        in_specs=[SMEM] + [VMEM] * (len(arrays) + 6),
        out_specs=(VMEM, VMEM),
        compiler_params=PARAMS,
        name="activations",
    )(me, *arrays, *weights, *sums)


def weight_grads(me, ring, width, features, cotangents, grads, hidden):
    arrays, table = gathered(features + cotangents)
    units = hidden.shape[0]

    def kernel(me_ref, *refs):
        grads_ref, hidden_ref, gate_ref, up_ref, down_ref = refs[len(arrays) :]
        for k, (number, column, owner) in enumerate(table):
            block = refs[number][:, column : column + width]
            start = lax.rem(me_ref[0] + owner % ring, ring) * width
            part = pl.ds(pl.multiple_of(start, width), width)
            if k < len(features):
                both = nn(grads_ref[...], block).astype(jnp.bfloat16)
                gate_ref[:, part] = both[:units]
                up_ref[:, part] = both[units:]
            else:
                down_ref[:, part] = nn(hidden_ref[...], block).astype(jnp.bfloat16)

    return pl.pallas_call(
        kernel,
        out_shape=[jax.ShapeDtypeStruct((units, ring * width), jnp.bfloat16)] * 3,
        in_specs=[SMEM] + [VMEM] * (len(arrays) + 2),
        out_specs=[VMEM] * 3,
        compiler_params=PARAMS,
        cost_estimate=pl.CostEstimate(flops=5 * 10**9, bytes_accessed=1000, transcendentals=0),
        name="weight_grads",
    )(me, *arrays, grads, hidden)


def local(tokens, cotangent, expert_ids, gate_values, w_gate, w_up, w_down):
    groups = lax.axis_size("ep")
    ring = lax.axis_size("tp")
    half = ring // 2
    near = half - 1
    tok_count, top_count = expert_ids.shape
    slots = max(2, tok_count * top_count * 4 // (groups * 3))
    width = tokens.shape[1]
    rows = groups * slots
    me = lax.axis_index("tp").astype(jnp.int32)
    me_ref = me.reshape(1)
    weights = (w_gate[0], w_up[0], w_down[0])

    def moved(value, by):
        return lax.ppermute(value, "tp", [(i, (i + by) % ring) for i in range(ring)])

    def over_ep(value):
        shape = (groups, slots, value.shape[1])
        value = lax.all_to_all(value.reshape(shape), "ep", split_axis=0, concat_axis=0, tiled=True)
        return value.reshape(rows, -1)

    ids, gates = expert_ids.T, gate_values.T
    sent, place = dispatch(ids, gates, [(tokens, False), (cotangent, True)], groups, slots)
    far_tokens, far_cot, sent = lax.optimization_barrier((tokens, cotangent, sent))
    mine = over_ep(sent)
    far_both = moved(jnp.concatenate([far_tokens, far_cot], axis=1), half)
    side_tokens = moved(far_tokens, -near)
    side_cot = moved(far_cot, near)
    far_sent, _ = dispatch(
        ids,
        gates,
        [
            (far_both[:, :width], False),
            (far_both[:, width:], True),
            (side_tokens, False),
            (side_cot, True),
        ],
        groups,
        slots,
    )
    x0, g0 = mine[:, :width], mine[:, width:]
    x0, g0, far_sent = lax.optimization_barrier((x0, g0, far_sent))
    x, g = {0: x0}, {0: g0}
    for step in range(1, near):
        for blocks in (x, g):
            blocks[-step] = moved(blocks[1 - step], 1)
            blocks[step] = moved(blocks[step - 1], -1)
    x[-near] = moved(x[1 - near], 1)
    g[near] = moved(g[near - 1], -1)
    far = over_ep(far_sent)

    early = [d for step in range(near) for d in ([-step, step] if step else [0])]
    early_x, early_g = [(x[d], 0, d) for d in early], [(g[d], 0, d) for d in early]
    late_x = [(far, 0, half), (far, 2 * width, near), (x[-near], 0, -near)]
    late_g = [(far, width, half), (far, 3 * width, -near), (g[near], 0, near)]
    sums = first_products(me_ref, ring, width, early_x, early_g, weights)
    grads, hidden = activations(me_ref, ring, width, late_x, late_g, weights, sums)

    paired = jnp.concatenate(weights[:2], axis=0)

    def columns(d):
        start = lax.rem(me + d % ring, np.int32(ring)) * width
        return lax.dynamic_slice_in_dim(paired, start, width, axis=1)

    def partial(d):
        return lax.optimization_barrier(tn(grads, columns(d)).astype(jnp.bfloat16))

    def added(*values):
        return sum(value.astype(jnp.float32) for value in values)

    away = [half, near, -near]
    right, left = partial(near - 1), partial(1 - near)
    side = jnp.concatenate([columns(d) for d in away], axis=1)
    far_back = over_ep(tn(grads, side).astype(jnp.bfloat16))
    for d in range(near - 2, -1, -1):
        right, left = moved(right, 1), moved(left, -1)
        if d:
            right = added(right, partial(d)).astype(jnp.bfloat16)
            left = added(left, partial(-d)).astype(jnp.bfloat16)
    total = added(partial(0), right, left).astype(jnp.bfloat16)

    grad_gate, grad_up, grad_down = weight_grads(
        me_ref, ring, width, early_x + late_x, early_g + late_g, grads, hidden
    )
    total, grad_gate, grad_up, grad_down = lax.optimization_barrier(
        (total, grad_gate, grad_up, grad_down)
    )
    back = over_ep(total)
    sides = tn(place, far_back).astype(jnp.bfloat16)
    sides = [moved(sides[:, k * width : (k + 1) * width], d) for k, d in enumerate(away)]
    input_grad = (tn(place, back) + added(*sides)).astype(jnp.bfloat16)
    return (input_grad, grad_gate[None], grad_up[None], grad_down[None])


def solution(mesh):
    in_specs = (
        P("ep", "tp"),
        P("ep", "tp"),
        P("ep", None),
        P("ep", None),
        P("ep", "tp", None),
        P("ep", "tp", None),
        P("ep", "tp", None),
    )
    out_specs = (P("ep", "tp"), P("ep", "tp", None), P("ep", "tp", None), P("ep", "tp", None))
    return jax.shard_map(local, mesh=mesh, in_specs=in_specs, out_specs=out_specs, check_vma=False)
```

```python
import jax
import jax.numpy as jnp
import numpy as np
from jax import lax
from jax.experimental import pallas as pl
from jax.experimental.pallas import tpu as pltpu
from jax.sharding import PartitionSpec as P

VMEM = pl.BlockSpec(memory_space=pltpu.VMEM)
SMEM = pl.BlockSpec(memory_space=pltpu.SMEM)
PARAMS = pltpu.CompilerParams(vmem_limit_bytes=56 * 1024 * 1024)


def nt(left, right):
    return lax.dot_general(left, right, (((1,), (1,)), ((), ())), preferred_element_type=jnp.float32)


def tn(left, right):
    return lax.dot_general(left, right, (((0,), (0,)), ((), ())), preferred_element_type=jnp.float32)


def nn(left, right):
    return jnp.dot(left, right, preferred_element_type=jnp.float32)


def dispatch(ids, gates, pieces, experts, slots):
    top, tokens = ids.shape
    count = experts * slots
    widths = [piece.shape[1] for piece, _ in pieces]
    scaled = [flag for _, flag in pieces]

    def kernel(ids_ref, gates_ref, *refs):
        rows_ref, place_ref = refs[-2:]
        ids = ids_ref[...]
        gates = gates_ref[...]
        expert = lax.broadcasted_iota(jnp.int32, (experts, tokens), 0)
        named = jnp.zeros((experts, tokens), jnp.float32)
        gate = jnp.zeros((experts, tokens), jnp.float32)
        for k in range(top):
            hit = ids[k : k + 1, :] == expert
            named = jnp.where(hit, 1.0, named)
            gate = jnp.where(hit, gates[k : k + 1, :], gate)
        earlier = (
            lax.broadcasted_iota(jnp.int32, (tokens, tokens), 0)
            < lax.broadcasted_iota(jnp.int32, (tokens, tokens), 1)
        ).astype(jnp.float32)
        before = nn(named.astype(jnp.bfloat16), earlier.astype(jnp.bfloat16))
        slot = jnp.where(named > 0.0, before, -1.0)
        shape = (experts, slots, tokens)
        wanted = lax.broadcasted_iota(jnp.int32, shape, 1).astype(jnp.float32)
        match = jnp.broadcast_to(slot[:, None, :], shape) == wanted
        scale = jnp.where(match, jnp.broadcast_to(gate[:, None, :], shape), 0.0)
        scale = jnp.sum(scale.reshape(count, tokens), axis=1, keepdims=True)
        place = match.astype(jnp.float32).reshape(count, tokens).astype(jnp.bfloat16)
        place_ref[...] = place
        at = 0
        for k, ref in enumerate(refs[:-2]):
            rows = nn(place, ref[...])
            if scaled[k]:
                rows = scale * rows
            rows_ref[:, at : at + widths[k]] = rows.astype(jnp.bfloat16)
            at += widths[k]

    return pl.pallas_call(
        kernel,
        out_shape=(
            jax.ShapeDtypeStruct((count, sum(widths)), jnp.bfloat16),
            jax.ShapeDtypeStruct((count, tokens), jnp.bfloat16),
        ),
        in_specs=[VMEM] * (2 + len(pieces)),
        out_specs=(VMEM, VMEM),
        compiler_params=PARAMS,
        name="dispatch",
    )(ids, gates, *[piece for piece, _ in pieces])


def gathered(terms):
    arrays, table = [], []
    for array, column, owner in terms:
        known = [k for k, other in enumerate(arrays) if other is array]
        if not known:
            arrays.append(array)
        table.append((known[0] if known else len(arrays) - 1, column, owner))
    return arrays, table


def first_products(me, ring, width, features, cotangents, weights, sums=(), flops=0):
    arrays, table = gathered(features + cotangents)
    rows = arrays[0].shape[0]
    units = weights[0].shape[0]

    def kernel(me_ref, *refs):
        w_gate, w_up, w_down = refs[len(arrays) : len(arrays) + 3]
        a_ref, b_ref, dh_ref = refs[-3:]
        if sums:
            for into, held in zip(refs[-3:], refs[-6:-3]):
                into[...] = held[...]
        for k, (number, column, owner) in enumerate(table):
            block = refs[number][:, column : column + width]
            start = lax.rem(me_ref[0] + owner % ring, ring) * width
            part = pl.ds(pl.multiple_of(start, width), width)
            if k == 0 and not sums:
                a_ref[...], b_ref[...] = nt(w_gate[:, part], block), nt(w_up[:, part], block)
            elif k < len(features):
                a_ref[...] += nt(w_gate[:, part], block)
                b_ref[...] += nt(w_up[:, part], block)
            elif k == len(features) and not sums:
                dh_ref[...] = nt(w_down[:, part], block)
            else:
                dh_ref[...] += nt(w_down[:, part], block)

    return pl.pallas_call(
        kernel,
        out_shape=[jax.ShapeDtypeStruct((units, rows), jnp.float32)] * 3,
        in_specs=[SMEM] + [VMEM] * (len(arrays) + 3 + len(sums)),
        out_specs=[VMEM] * 3,
        compiler_params=PARAMS,
        cost_estimate=pl.CostEstimate(flops=flops, bytes_accessed=1000, transcendentals=0),
        name="first_products",
    )(me, *arrays, *weights, *sums)


def activations(me, ring, width, features, cotangents, weights, sums, away):
    arrays, table = gathered(features + cotangents)
    rows = arrays[0].shape[0]
    units = weights[0].shape[0]

    def kernel(me_ref, *refs):
        w_gate, w_up, w_down, a_ref, b_ref, dh_ref = refs[len(arrays) : len(arrays) + 6]
        grads_ref, hidden_ref, away_ref = refs[len(arrays) + 6 :]
        a, b, dh = a_ref[...], b_ref[...], dh_ref[...]
        for k, (number, column, owner) in enumerate(table):
            block = refs[number][:, column : column + width]
            start = lax.rem(me_ref[0] + owner % ring, ring) * width
            part = pl.ds(pl.multiple_of(start, width), width)
            if k < len(features):
                a += nt(w_gate[:, part], block)
                b += nt(w_up[:, part], block)
            else:
                dh += nt(w_down[:, part], block)
        s = jax.nn.sigmoid(a)
        swish = a * s
        hidden_ref[...] = (swish * b).astype(jnp.bfloat16)
        grads_ref[:units, :] = (dh * b * s * (1.0 + a * (1.0 - s))).astype(jnp.bfloat16)
        grads_ref[units:, :] = (dh * swish).astype(jnp.bfloat16)
        for k, owner in enumerate(away):
            start = lax.rem(me_ref[0] + owner % ring, ring) * width
            part = pl.ds(pl.multiple_of(start, width), width)
            both = tn(grads_ref[:units, :], w_gate[:, part]) + tn(grads_ref[units:, :], w_up[:, part])
            away_ref[:, k * width : (k + 1) * width] = both.astype(jnp.bfloat16)

    return pl.pallas_call(
        kernel,
        out_shape=(
            jax.ShapeDtypeStruct((2 * units, rows), jnp.bfloat16),
            jax.ShapeDtypeStruct((units, rows), jnp.bfloat16),
            jax.ShapeDtypeStruct((rows, len(away) * width), jnp.bfloat16),
        ),
        in_specs=[SMEM] + [VMEM] * (len(arrays) + 6),
        out_specs=(VMEM, VMEM, VMEM),
        compiler_params=PARAMS,
        name="activations",
    )(me, *arrays, *weights, *sums)


def weight_grads(me, ring, width, features, cotangents, grads, hidden):
    arrays, table = gathered(features + cotangents)
    units = hidden.shape[0]

    def kernel(me_ref, *refs):
        grads_ref, hidden_ref, gate_ref, up_ref, down_ref = refs[len(arrays) :]
        for k, (number, column, owner) in enumerate(table):
            block = refs[number][:, column : column + width]
            start = lax.rem(me_ref[0] + owner % ring, ring) * width
            part = pl.ds(pl.multiple_of(start, width), width)
            if k < len(features):
                both = nn(grads_ref[...], block).astype(jnp.bfloat16)
                gate_ref[:, part] = both[:units]
                up_ref[:, part] = both[units:]
            else:
                down_ref[:, part] = nn(hidden_ref[...], block).astype(jnp.bfloat16)

    return pl.pallas_call(
        kernel,
        out_shape=[jax.ShapeDtypeStruct((units, ring * width), jnp.bfloat16)] * 3,
        in_specs=[SMEM] + [VMEM] * (len(arrays) + 2),
        out_specs=[VMEM] * 3,
        compiler_params=PARAMS,
        cost_estimate=pl.CostEstimate(flops=5 * 10**9, bytes_accessed=1000, transcendentals=0),
        name="weight_grads",
    )(me, *arrays, grads, hidden)


def local(tokens, cotangent, expert_ids, gate_values, w_gate, w_up, w_down):
    groups = lax.axis_size("ep")
    ring = lax.axis_size("tp")
    half = ring // 2
    near = half - 1
    tok_count, top_count = expert_ids.shape
    slots = max(2, tok_count * top_count * 4 // (groups * 3))
    width = tokens.shape[1]
    rows = groups * slots
    me = lax.axis_index("tp").astype(jnp.int32)
    me_ref = me.reshape(1)
    weights = (w_gate[0], w_up[0], w_down[0])

    def moved(value, by):
        return lax.ppermute(value, "tp", [(i, (i + by) % ring) for i in range(ring)])

    def over_ep(value):
        shape = (groups, slots, value.shape[1])
        value = lax.all_to_all(value.reshape(shape), "ep", split_axis=0, concat_axis=0, tiled=True)
        return value.reshape(rows, -1)

    ids, gates = expert_ids.T, gate_values.T
    sent, place = dispatch(ids, gates, [(tokens, False), (cotangent, True)], groups, slots)
    far_tokens, far_cot, sent = lax.optimization_barrier((tokens, cotangent, sent))
    mine = over_ep(sent)
    far_both = moved(jnp.concatenate([far_tokens, far_cot], axis=1), half)
    side_tokens = moved(far_tokens, -near)
    side_cot = moved(far_cot, near)
    far_sent, _ = dispatch(
        ids,
        gates,
        [
            (far_both[:, :width], False),
            (far_both[:, width:], True),
            (side_tokens, False),
            (side_cot, True),
        ],
        groups,
        slots,
    )
    x0, g0 = mine[:, :width], mine[:, width:]
    x0, g0, far_sent = lax.optimization_barrier((x0, g0, far_sent))
    x, g = {0: x0}, {0: g0}
    for step in range(1, near):
        for blocks in (x, g):
            blocks[-step] = moved(blocks[1 - step], 1)
            blocks[step] = moved(blocks[step - 1], -1)
    x[-near] = moved(x[1 - near], 1)
    g[near] = moved(g[near - 1], -1)
    far = over_ep(far_sent)

    early = [d for step in range(near) for d in ([-step, step] if step else [0])]
    early_x, early_g = [(x[d], 0, d) for d in early], [(g[d], 0, d) for d in early]
    last_x, last_g = [(x[-near], 0, -near)], [(g[near], 0, near)]
    late_x = [(far, 0, half), (far, 2 * width, near)]
    late_g = [(far, width, half), (far, 3 * width, -near)]
    sums = first_products(me_ref, ring, width, early_x, early_g, weights, flops=3400 * 10**7)
    sums = first_products(me_ref, ring, width, last_x, last_g, weights, sums, flops=10**9)
    away = [half, near, -near]
    grads, hidden, side = activations(me_ref, ring, width, late_x, late_g, weights, sums, away)

    paired = jnp.concatenate(weights[:2], axis=0)

    def columns(d):
        start = lax.rem(me + d % ring, np.int32(ring)) * width
        return lax.dynamic_slice_in_dim(paired, start, width, axis=1)

    def partial(d):
        return lax.optimization_barrier(tn(grads, columns(d)).astype(jnp.bfloat16))

    def added(*values):
        return sum(value.astype(jnp.float32) for value in values)

    right, left = partial(near - 1), partial(1 - near)
    far_back = over_ep(side)
    for d in range(near - 2, -1, -1):
        right, left = moved(right, 1), moved(left, -1)
        if d:
            right = added(right, partial(d)).astype(jnp.bfloat16)
            left = added(left, partial(-d)).astype(jnp.bfloat16)
    total = added(partial(0), right, left).astype(jnp.bfloat16)

    grad_gate, grad_up, grad_down = weight_grads(
        me_ref, ring, width, early_x + last_x + late_x, early_g + last_g + late_g, grads, hidden
    )
    total, grad_gate, grad_up, grad_down = lax.optimization_barrier(
        (total, grad_gate, grad_up, grad_down)
    )
    back = over_ep(total)
    sides = tn(place, far_back).astype(jnp.bfloat16)
    sides = [moved(sides[:, k * width : (k + 1) * width], d) for k, d in enumerate(away)]
    input_grad = (tn(place, back) + added(*sides)).astype(jnp.bfloat16)
    return (input_grad, grad_gate[None], grad_up[None], grad_down[None])


def solution(mesh):
    in_specs = (
        P("ep", "tp"),
        P("ep", "tp"),
        P("ep", None),
        P("ep", None),
        P("ep", "tp", None),
        P("ep", "tp", None),
        P("ep", "tp", None),
    )
    out_specs = (P("ep", "tp"), P("ep", "tp", None), P("ep", "tp", None), P("ep", "tp", None))
    return jax.shard_map(local, mesh=mesh, in_specs=in_specs, out_specs=out_specs, check_vma=False)
```

```python
import jax
import jax.numpy as jnp
import numpy as np
from jax import lax
from jax.experimental import pallas as pl
from jax.experimental.pallas import tpu as pltpu
from jax.sharding import PartitionSpec as P

VMEM = pl.BlockSpec(memory_space=pltpu.VMEM)
SMEM = pl.BlockSpec(memory_space=pltpu.SMEM)
PARAMS = pltpu.CompilerParams(vmem_limit_bytes=62 * 1024 * 1024)


def nt(left, right):
    return lax.dot_general(left, right, (((1,), (1,)), ((), ())), preferred_element_type=jnp.float32)


def tn(left, right):
    return lax.dot_general(left, right, (((0,), (0,)), ((), ())), preferred_element_type=jnp.float32)


def nn(left, right):
    return jnp.dot(left, right, preferred_element_type=jnp.float32)


def dispatch(ids, gates, pieces, experts, slots):
    top, tokens = ids.shape
    count = experts * slots
    widths = [piece.shape[1] for piece, _ in pieces]
    scaled = [flag for _, flag in pieces]

    def kernel(ids_ref, gates_ref, *refs):
        rows_ref, place_ref = refs[-2:]
        ids = ids_ref[...]
        gates = gates_ref[...]
        expert = lax.broadcasted_iota(jnp.int32, (experts, tokens), 0)
        named = jnp.zeros((experts, tokens), jnp.float32)
        gate = jnp.zeros((experts, tokens), jnp.float32)
        for k in range(top):
            hit = ids[k : k + 1, :] == expert
            named = jnp.where(hit, 1.0, named)
            gate = jnp.where(hit, gates[k : k + 1, :], gate)
        earlier = (
            lax.broadcasted_iota(jnp.int32, (tokens, tokens), 0)
            < lax.broadcasted_iota(jnp.int32, (tokens, tokens), 1)
        ).astype(jnp.float32)
        before = nn(named.astype(jnp.bfloat16), earlier.astype(jnp.bfloat16))
        slot = jnp.where(named > 0.0, before, -1.0)
        shape = (experts, slots, tokens)
        wanted = lax.broadcasted_iota(jnp.int32, shape, 1).astype(jnp.float32)
        match = jnp.broadcast_to(slot[:, None, :], shape) == wanted
        scale = jnp.where(match, jnp.broadcast_to(gate[:, None, :], shape), 0.0)
        scale = jnp.sum(scale.reshape(count, tokens), axis=1, keepdims=True)
        place = match.astype(jnp.float32).reshape(count, tokens).astype(jnp.bfloat16)
        place_ref[...] = place
        at = 0
        for k, ref in enumerate(refs[:-2]):
            rows = nn(place, ref[...])
            if scaled[k]:
                rows = scale * rows
            rows_ref[:, at : at + widths[k]] = rows.astype(jnp.bfloat16)
            at += widths[k]

    return pl.pallas_call(
        kernel,
        out_shape=(
            jax.ShapeDtypeStruct((count, sum(widths)), jnp.bfloat16),
            jax.ShapeDtypeStruct((count, tokens), jnp.bfloat16),
        ),
        in_specs=[VMEM] * (2 + len(pieces)),
        out_specs=(VMEM, VMEM),
        compiler_params=PARAMS,
        name="dispatch",
    )(ids, gates, *[piece for piece, _ in pieces])


def gathered(terms):
    arrays, table = [], []
    for array, column, owner in terms:
        known = [k for k, other in enumerate(arrays) if other is array]
        if not known:
            arrays.append(array)
        table.append((known[0] if known else len(arrays) - 1, column, owner))
    return arrays, table


def first_products(me, ring, width, features, cotangents, weights):
    arrays, table = gathered(features + cotangents)
    rows = arrays[0].shape[0]
    units = weights[0].shape[0]

    def kernel(me_ref, *refs):
        w_gate, w_up, w_down, a_ref, b_ref, dh_ref = refs[len(arrays) :]
        for k, (number, column, owner) in enumerate(table):
            block = refs[number][:, column : column + width]
            start = lax.rem(me_ref[0] + owner % ring, ring) * width
            part = pl.ds(pl.multiple_of(start, width), width)
            if k == 0:
                a_ref[...], b_ref[...] = nt(w_gate[:, part], block), nt(w_up[:, part], block)
            elif k < len(features):
                a_ref[...] += nt(w_gate[:, part], block)
                b_ref[...] += nt(w_up[:, part], block)
            elif k == len(features):
                dh_ref[...] = nt(w_down[:, part], block)
            else:
                dh_ref[...] += nt(w_down[:, part], block)

    return pl.pallas_call(
        kernel,
        out_shape=[jax.ShapeDtypeStruct((units, rows), jnp.float32)] * 3,
        in_specs=[SMEM] + [VMEM] * (len(arrays) + 3),
        out_specs=[VMEM] * 3,
        compiler_params=PARAMS,
        cost_estimate=pl.CostEstimate(flops=32857 * 10**6, bytes_accessed=1000, transcendentals=0),
        name="first_products",
    )(me, *arrays, *weights)


def activations(me, ring, width, features, cotangents, weights, sums, away):
    arrays, table = gathered(features + cotangents)
    rows = arrays[0].shape[0]
    units = weights[0].shape[0]

    def kernel(me_ref, *refs):
        w_gate, w_up, w_down, a_ref, b_ref, dh_ref = refs[len(arrays) : len(arrays) + 6]
        grads_ref, hidden_ref, away_ref = refs[len(arrays) + 6 :]
        a, b, dh = a_ref[...], b_ref[...], dh_ref[...]
        for k, (number, column, owner) in enumerate(table):
            block = refs[number][:, column : column + width]
            start = lax.rem(me_ref[0] + owner % ring, ring) * width
            part = pl.ds(pl.multiple_of(start, width), width)
            if k < len(features):
                a += nt(w_gate[:, part], block)
                b += nt(w_up[:, part], block)
            else:
                dh += nt(w_down[:, part], block)
        s = jax.nn.sigmoid(a)
        swish = a * s
        hidden_ref[...] = (swish * b).astype(jnp.bfloat16)
        grads_ref[:units, :] = (dh * b * s * (1.0 + a * (1.0 - s))).astype(jnp.bfloat16)
        grads_ref[units:, :] = (dh * swish).astype(jnp.bfloat16)
        for k, owner in enumerate(away):
            start = lax.rem(me_ref[0] + owner % ring, ring) * width
            part = pl.ds(pl.multiple_of(start, width), width)
            both = tn(grads_ref[:units, :], w_gate[:, part]) + tn(grads_ref[units:, :], w_up[:, part])
            away_ref[:, k * width : (k + 1) * width] = both.astype(jnp.bfloat16)

    return pl.pallas_call(
        kernel,
        out_shape=(
            jax.ShapeDtypeStruct((2 * units, rows), jnp.bfloat16),
            jax.ShapeDtypeStruct((units, rows), jnp.bfloat16),
            jax.ShapeDtypeStruct((rows, len(away) * width), jnp.bfloat16),
        ),
        in_specs=[SMEM] + [VMEM] * (len(arrays) + 6),
        out_specs=(VMEM, VMEM, VMEM),
        compiler_params=PARAMS,
        name="activations",
    )(me, *arrays, *weights, *sums)


def weight_grads(me, ring, width, features, cotangents, grads, hidden):
    arrays, table = gathered(features + cotangents)
    units = hidden.shape[0]

    def kernel(me_ref, *refs):
        grads_ref, hidden_ref, gate_ref, up_ref, down_ref = refs[len(arrays) :]
        for k, (number, column, owner) in enumerate(table):
            block = refs[number][:, column : column + width]
            start = lax.rem(me_ref[0] + owner % ring, ring) * width
            part = pl.ds(pl.multiple_of(start, width), width)
            if k < len(features):
                both = nn(grads_ref[...], block).astype(jnp.bfloat16)
                gate_ref[:, part] = both[:units]
                up_ref[:, part] = both[units:]
            else:
                down_ref[:, part] = nn(hidden_ref[...], block).astype(jnp.bfloat16)

    return pl.pallas_call(
        kernel,
        out_shape=[jax.ShapeDtypeStruct((units, ring * width), jnp.bfloat16)] * 3,
        in_specs=[SMEM] + [VMEM] * (len(arrays) + 2),
        out_specs=[VMEM] * 3,
        compiler_params=PARAMS,
        cost_estimate=pl.CostEstimate(flops=5 * 10**9, bytes_accessed=1000, transcendentals=0),
        name="weight_grads",
    )(me, *arrays, grads, hidden)


def local(tokens, cotangent, expert_ids, gate_values, w_gate, w_up, w_down):
    groups = lax.axis_size("ep")
    ring = lax.axis_size("tp")
    half = ring // 2
    near = half - 1
    tok_count, top_count = expert_ids.shape
    slots = max(2, tok_count * top_count * 4 // (groups * 3))
    width = tokens.shape[1]
    rows = groups * slots
    me = lax.axis_index("tp").astype(jnp.int32)
    me_ref = me.reshape(1)
    weights = (w_gate[0], w_up[0], w_down[0])

    def moved(value, by):
        return lax.ppermute(value, "tp", [(i, (i + by) % ring) for i in range(ring)])

    def over_ep(value):
        shape = (groups, slots, value.shape[1])
        value = lax.all_to_all(value.reshape(shape), "ep", split_axis=0, concat_axis=0, tiled=True)
        return value.reshape(rows, -1)

    ids, gates = expert_ids.T, gate_values.T
    sent, place = dispatch(ids, gates, [(tokens, False), (cotangent, True)], groups, slots)
    far_tokens, far_cot, sent = lax.optimization_barrier((tokens, cotangent, sent))
    mine = over_ep(sent)
    far_both = moved(jnp.concatenate([far_tokens, far_cot], axis=1), half)
    side_tokens = moved(far_tokens, -near)
    side_cot = moved(far_cot, near)
    far_sent, _ = dispatch(
        ids,
        gates,
        [
            (far_both[:, :width], False),
            (far_both[:, width:], True),
            (side_tokens, False),
            (side_cot, True),
        ],
        groups,
        slots,
    )
    x0, g0 = mine[:, :width], mine[:, width:]
    x0, g0, far_sent = lax.optimization_barrier((x0, g0, far_sent))
    x, g = {0: x0}, {0: g0}
    for step in range(1, near):
        for blocks in (x, g):
            blocks[-step] = moved(blocks[1 - step], 1)
            blocks[step] = moved(blocks[step - 1], -1)
    x[-near] = moved(x[1 - near], 1)
    g[near] = moved(g[near - 1], -1)
    far = over_ep(far_sent)

    early = [d for step in range(near) for d in ([-step, step] if step else [0])]
    early_x, early_g = [(x[d], 0, d) for d in early], [(g[d], 0, d) for d in early]
    late_x = [(far, 0, half), (far, 2 * width, near), (x[-near], 0, -near)]
    late_g = [(far, width, half), (far, 3 * width, -near), (g[near], 0, near)]
    sums = first_products(me_ref, ring, width, early_x, early_g, weights)
    away = [half, near, -near]
    grads, hidden, side = activations(me_ref, ring, width, late_x, late_g, weights, sums, away)

    paired = jnp.concatenate(weights[:2], axis=0)

    def columns(d):
        start = lax.rem(me + d % ring, np.int32(ring)) * width
        return lax.dynamic_slice_in_dim(paired, start, width, axis=1)

    def partial(d):
        return lax.optimization_barrier(tn(grads, columns(d)).astype(jnp.bfloat16))

    def added(*values):
        return sum(value.astype(jnp.float32) for value in values)

    right, left = partial(near - 1), partial(1 - near)
    far_back = over_ep(side)
    for d in range(near - 2, -1, -1):
        right, left = moved(right, 1), moved(left, -1)
        if d:
            right = added(right, partial(d)).astype(jnp.bfloat16)
            left = added(left, partial(-d)).astype(jnp.bfloat16)
    total = added(partial(0), right, left).astype(jnp.bfloat16)

    grad_gate, grad_up, grad_down = weight_grads(
        me_ref, ring, width, early_x + late_x, early_g + late_g, grads, hidden
    )
    total, grad_gate, grad_up, grad_down = lax.optimization_barrier(
        (total, grad_gate, grad_up, grad_down)
    )
    back = over_ep(total)
    sides = tn(place, far_back).astype(jnp.bfloat16)
    sides = [moved(sides[:, k * width : (k + 1) * width], d) for k, d in enumerate(away)]
    input_grad = (tn(place, back) + added(*sides)).astype(jnp.bfloat16)
    return (input_grad, grad_gate[None], grad_up[None], grad_down[None])


def solution(mesh):
    in_specs = (
        P("ep", "tp"),
        P("ep", "tp"),
        P("ep", None),
        P("ep", None),
        P("ep", "tp", None),
        P("ep", "tp", None),
        P("ep", "tp", None),
    )
    out_specs = (P("ep", "tp"), P("ep", "tp", None), P("ep", "tp", None), P("ep", "tp", None))
    return jax.shard_map(local, mesh=mesh, in_specs=in_specs, out_specs=out_specs, check_vma=False)
```

```python
import jax
import jax.numpy as jnp
import numpy as np
from jax import lax
from jax.experimental import pallas as pl
from jax.experimental.pallas import tpu as pltpu
from jax.sharding import PartitionSpec as P

VMEM = pl.BlockSpec(memory_space=pltpu.VMEM)
SMEM = pl.BlockSpec(memory_space=pltpu.SMEM)
PARAMS = pltpu.CompilerParams(vmem_limit_bytes=62 * 1024 * 1024)


def nt(left, right):
    return lax.dot_general(left, right, (((1,), (1,)), ((), ())), preferred_element_type=jnp.float32)


def tn(left, right):
    return lax.dot_general(left, right, (((0,), (0,)), ((), ())), preferred_element_type=jnp.float32)


def nn(left, right):
    return jnp.dot(left, right, preferred_element_type=jnp.float32)


def dispatch(ids, gates, pieces, experts, slots):
    top, tokens = ids.shape
    count = experts * slots
    widths = [piece.shape[1] for piece, _ in pieces]
    scaled = [flag for _, flag in pieces]

    def kernel(ids_ref, gates_ref, *refs):
        rows_ref, place_ref = refs[-2:]
        ids = ids_ref[...]
        gates = gates_ref[...]
        expert = lax.broadcasted_iota(jnp.int32, (experts, tokens), 0)
        named = jnp.zeros((experts, tokens), jnp.float32)
        gate = jnp.zeros((experts, tokens), jnp.float32)
        for k in range(top):
            hit = ids[k : k + 1, :] == expert
            named = jnp.where(hit, 1.0, named)
            gate = jnp.where(hit, gates[k : k + 1, :], gate)
        earlier = (
            lax.broadcasted_iota(jnp.int32, (tokens, tokens), 0)
            < lax.broadcasted_iota(jnp.int32, (tokens, tokens), 1)
        ).astype(jnp.float32)
        before = nn(named.astype(jnp.bfloat16), earlier.astype(jnp.bfloat16))
        slot = jnp.where(named > 0.0, before, -1.0)
        shape = (experts, slots, tokens)
        wanted = lax.broadcasted_iota(jnp.int32, shape, 1).astype(jnp.float32)
        match = jnp.broadcast_to(slot[:, None, :], shape) == wanted
        scale = jnp.where(match, jnp.broadcast_to(gate[:, None, :], shape), 0.0)
        scale = jnp.sum(scale.reshape(count, tokens), axis=1, keepdims=True)
        place = match.astype(jnp.float32).reshape(count, tokens).astype(jnp.bfloat16)
        place_ref[...] = place
        at = 0
        for k, ref in enumerate(refs[:-2]):
            rows = nn(place, ref[...])
            if scaled[k]:
                rows = scale * rows
            rows_ref[:, at : at + widths[k]] = rows.astype(jnp.bfloat16)
            at += widths[k]

    return pl.pallas_call(
        kernel,
        out_shape=(
            jax.ShapeDtypeStruct((count, sum(widths)), jnp.bfloat16),
            jax.ShapeDtypeStruct((count, tokens), jnp.bfloat16),
        ),
        in_specs=[VMEM] * (2 + len(pieces)),
        out_specs=(VMEM, VMEM),
        compiler_params=PARAMS,
        name="dispatch",
    )(ids, gates, *[piece for piece, _ in pieces])


def gathered(terms):
    arrays, table = [], []
    for array, column, owner in terms:
        known = [k for k, other in enumerate(arrays) if other is array]
        if not known:
            arrays.append(array)
        table.append((known[0] if known else len(arrays) - 1, column, owner))
    return arrays, table


def first_products(me, ring, width, features, cotangents, weights, sums=(), flops=0):
    arrays, table = gathered(features + cotangents)
    rows = arrays[0].shape[0]
    units = weights[0].shape[0]

    def kernel(me_ref, *refs):
        w_gate, w_up, w_down = refs[len(arrays) : len(arrays) + 3]
        a_ref, b_ref, dh_ref = refs[-3:]
        if sums:
            for into, held in zip(refs[-3:], refs[-6:-3]):
                into[...] = held[...]
        for k, (number, column, owner) in enumerate(table):
            block = refs[number][:, column : column + width]
            start = lax.rem(me_ref[0] + owner % ring, ring) * width
            part = pl.ds(pl.multiple_of(start, width), width)
            if k == 0 and not sums:
                a_ref[...], b_ref[...] = nt(w_gate[:, part], block), nt(w_up[:, part], block)
            elif k < len(features):
                a_ref[...] += nt(w_gate[:, part], block)
                b_ref[...] += nt(w_up[:, part], block)
            elif k == len(features) and not sums:
                dh_ref[...] = nt(w_down[:, part], block)
            else:
                dh_ref[...] += nt(w_down[:, part], block)

    return pl.pallas_call(
        kernel,
        out_shape=[jax.ShapeDtypeStruct((units, rows), jnp.float32)] * 3,
        in_specs=[SMEM] + [VMEM] * (len(arrays) + 3 + len(sums)),
        out_specs=[VMEM] * 3,
        compiler_params=PARAMS,
        cost_estimate=pl.CostEstimate(flops=flops, bytes_accessed=1000, transcendentals=0),
        name="first_products",
    )(me, *arrays, *weights, *sums)


def activations(me, ring, width, features, cotangents, weights, sums, away):
    arrays, table = gathered(features + cotangents)
    rows = arrays[0].shape[0]
    units = weights[0].shape[0]

    def kernel(me_ref, *refs):
        w_gate, w_up, w_down, a_ref, b_ref, dh_ref = refs[len(arrays) : len(arrays) + 6]
        grads_ref, hidden_ref, away_ref = refs[len(arrays) + 6 :]
        a, b, dh = a_ref[...], b_ref[...], dh_ref[...]
        for k, (number, column, owner) in enumerate(table):
            block = refs[number][:, column : column + width]
            start = lax.rem(me_ref[0] + owner % ring, ring) * width
            part = pl.ds(pl.multiple_of(start, width), width)
            if k < len(features):
                a += nt(w_gate[:, part], block)
                b += nt(w_up[:, part], block)
            else:
                dh += nt(w_down[:, part], block)
        s = jax.nn.sigmoid(a)
        swish = a * s
        hidden_ref[...] = (swish * b).astype(jnp.bfloat16)
        grads_ref[:units, :] = (dh * b * s * (1.0 + a * (1.0 - s))).astype(jnp.bfloat16)
        grads_ref[units:, :] = (dh * swish).astype(jnp.bfloat16)
        for k, owner in enumerate(away):
            start = lax.rem(me_ref[0] + owner % ring, ring) * width
            part = pl.ds(pl.multiple_of(start, width), width)
            both = tn(grads_ref[:units, :], w_gate[:, part]) + tn(grads_ref[units:, :], w_up[:, part])
            away_ref[:, k * width : (k + 1) * width] = both.astype(jnp.bfloat16)

    return pl.pallas_call(
        kernel,
        out_shape=(
            jax.ShapeDtypeStruct((2 * units, rows), jnp.bfloat16),
            jax.ShapeDtypeStruct((units, rows), jnp.bfloat16),
            jax.ShapeDtypeStruct((rows, len(away) * width), jnp.bfloat16),
        ),
        in_specs=[SMEM] + [VMEM] * (len(arrays) + 6),
        out_specs=(VMEM, VMEM, VMEM),
        compiler_params=PARAMS,
        name="activations",
    )(me, *arrays, *weights, *sums)


def weight_grads(me, ring, width, features, cotangents, grads, hidden):
    arrays, table = gathered(features + cotangents)
    units = hidden.shape[0]

    def kernel(me_ref, *refs):
        grads_ref, hidden_ref, gate_ref, up_ref, down_ref = refs[len(arrays) :]
        for k, (number, column, owner) in enumerate(table):
            block = refs[number][:, column : column + width]
            start = lax.rem(me_ref[0] + owner % ring, ring) * width
            part = pl.ds(pl.multiple_of(start, width), width)
            if k < len(features):
                both = nn(grads_ref[...], block).astype(jnp.bfloat16)
                gate_ref[:, part] = both[:units]
                up_ref[:, part] = both[units:]
            else:
                down_ref[:, part] = nn(hidden_ref[...], block).astype(jnp.bfloat16)

    return pl.pallas_call(
        kernel,
        out_shape=[jax.ShapeDtypeStruct((units, ring * width), jnp.bfloat16)] * 3,
        in_specs=[SMEM] + [VMEM] * (len(arrays) + 2),
        out_specs=[VMEM] * 3,
        compiler_params=PARAMS,
        cost_estimate=pl.CostEstimate(flops=5 * 10**9, bytes_accessed=1000, transcendentals=0),
        name="weight_grads",
    )(me, *arrays, grads, hidden)


def local(tokens, cotangent, expert_ids, gate_values, w_gate, w_up, w_down):
    groups = lax.axis_size("ep")
    ring = lax.axis_size("tp")
    half = ring // 2
    near = half - 1
    tok_count, top_count = expert_ids.shape
    slots = max(2, tok_count * top_count * 4 // (groups * 3))
    width = tokens.shape[1]
    rows = groups * slots
    me = lax.axis_index("tp").astype(jnp.int32)
    me_ref = me.reshape(1)
    weights = (w_gate[0], w_up[0], w_down[0])

    def moved(value, by):
        return lax.ppermute(value, "tp", [(i, (i + by) % ring) for i in range(ring)])

    def over_ep(value):
        shape = (groups, slots, value.shape[1])
        value = lax.all_to_all(value.reshape(shape), "ep", split_axis=0, concat_axis=0, tiled=True)
        return value.reshape(rows, -1)

    ids, gates = expert_ids.T, gate_values.T
    sent, place = dispatch(ids, gates, [(tokens, False), (cotangent, True)], groups, slots)
    far_tokens, far_cot, sent = lax.optimization_barrier((tokens, cotangent, sent))
    mine = over_ep(sent)
    far_both = moved(jnp.concatenate([far_tokens, far_cot], axis=1), half)
    side_tokens = moved(far_tokens, -near)
    side_cot = moved(far_cot, near)
    far_sent, _ = dispatch(
        ids,
        gates,
        [
            (far_both[:, :width], False),
            (far_both[:, width:], True),
            (side_tokens, False),
            (side_cot, True),
        ],
        groups,
        slots,
    )
    x0, g0 = mine[:, :width], mine[:, width:]
    x0, g0, far_sent = lax.optimization_barrier((x0, g0, far_sent))
    x, g = {0: x0}, {0: g0}
    for step in range(1, near):
        for blocks in (x, g):
            blocks[-step] = moved(blocks[1 - step], 1)
            blocks[step] = moved(blocks[step - 1], -1)
    x[-near] = moved(x[1 - near], 1)
    g[near] = moved(g[near - 1], -1)
    far = over_ep(far_sent)

    early = [d for step in range(near) for d in ([-step, step] if step else [0])]
    early_x, early_g = [(x[d], 0, d) for d in early], [(g[d], 0, d) for d in early]
    last_x, last_g = [(x[-near], 0, -near)], [(g[near], 0, near)]
    late_x = [(far, 0, half), (far, 2 * width, near)]
    late_g = [(far, width, half), (far, 3 * width, -near)]
    sums = first_products(me_ref, ring, width, early_x, early_g, weights, flops=3400 * 10**7)
    sums = first_products(me_ref, ring, width, last_x, last_g, weights, sums, flops=10**9)
    away = [half, near, -near]
    grads, hidden, side = activations(me_ref, ring, width, late_x, late_g, weights, sums, away)

    paired = jnp.concatenate(weights[:2], axis=0)

    def columns(d):
        start = lax.rem(me + d % ring, np.int32(ring)) * width
        return lax.dynamic_slice_in_dim(paired, start, width, axis=1)

    def partial(d):
        return lax.optimization_barrier(tn(grads, columns(d)).astype(jnp.bfloat16))

    def added(*values):
        return sum(value.astype(jnp.float32) for value in values)

    right, left = partial(near - 1), partial(1 - near)
    far_back = over_ep(side)
    for d in range(near - 2, -1, -1):
        right, left = moved(right, 1), moved(left, -1)
        if d:
            right = added(right, partial(d)).astype(jnp.bfloat16)
            left = added(left, partial(-d)).astype(jnp.bfloat16)
    total = added(partial(0), right, left).astype(jnp.bfloat16)

    grad_gate, grad_up, grad_down = weight_grads(
        me_ref, ring, width, early_x + last_x + late_x, early_g + last_g + late_g, grads, hidden
    )
    total, grad_gate, grad_up, grad_down = lax.optimization_barrier(
        (total, grad_gate, grad_up, grad_down)
    )
    back = over_ep(total)
    sides = tn(place, far_back).astype(jnp.bfloat16)
    sides = [moved(sides[:, k * width : (k + 1) * width], d) for k, d in enumerate(away)]
    input_grad = (tn(place, back) + added(*sides)).astype(jnp.bfloat16)
    return (input_grad, grad_gate[None], grad_up[None], grad_down[None])


def solution(mesh):
    in_specs = (
        P("ep", "tp"),
        P("ep", "tp"),
        P("ep", None),
        P("ep", None),
        P("ep", "tp", None),
        P("ep", "tp", None),
        P("ep", "tp", None),
    )
    out_specs = (P("ep", "tp"), P("ep", "tp", None), P("ep", "tp", None), P("ep", "tp", None))
    return jax.shard_map(local, mesh=mesh, in_specs=in_specs, out_specs=out_specs, check_vma=False)
```
